32 devices in a mesh: row: 8 (over z, y), col: 4 (over x, core).
Axes of the slice: x: 2, y: 2, z: 4, core: 2. Of those that a mesh axis runs over, the one named last changes fastest.
Arguments:
- solved: bfloat16 [4096, 4096], P('col', 'row'), may hold values from -6 to 6
- factor_rows: bfloat16 [1024, 4096], P(None, 'col'), may hold values from -0.09375 to 0.09375
- diag_inverse: bfloat16 [1024, 1024], replicated, may hold values from -1 to 1, as said below
- features: bfloat16 [4096, 1024], P('row'), may hold values from -6 to 6
- covariance: float32 [4096, 4096], P('row', 'col'), may hold values from -6 to 6
Outputs:
- cov_out: float32 [4096, 4096], P('row', 'col')
The draws below stay inside these ranges and needn't reach their ends.
Inputs may be any that keep to these rules, and one draw needn't show every extreme that they name: diag_inverse is lower triangular; its diagonal lies between 1 / sqrt(1024) and 3 / sqrt(1024).
All inputs are finite; a program needn't handle non-finite values.
Results may differ from the reference program's by a relative error of at most 0.0018.
Values may be sent and summed in bfloat16 or wider, within the bound.
No kernel may reach another device: no remote copies, remote signals or barrier semaphores. Data moves between devices by JAX's collectives and lax.ppermute only.
A program may use at most 128 MiB of HBM per device.

```python
import jax
import jax.numpy as jnp
from jax import lax

B = 1024
K0 = 4096
N = 4096


def draw_diag_inverse(key, part):
    base = jax.random.fold_in(key, 7)
    first, second = jax.random.split(base)
    diagonal = jax.random.uniform(first, (B,), jnp.float32, 1.0, 3.0)
    lower = jax.random.normal(second, (B, B), jnp.float32) / jnp.sqrt(jnp.float32(B))
    matrix = jnp.tril(lower, -1) + jnp.diag(diagonal)
    return (matrix / jnp.sqrt(jnp.float32(B))).astype(jnp.bfloat16)


def level_of(key, dims, cuts, smallest, top_value):
    factor_of = 1.0
    for dim, parts in cuts:
        steps = jax.random.uniform(jax.random.fold_in(jax.random.fold_in(key, 6), dim), (parts,), jnp.float32, smallest / len(cuts), top_value / len(cuts))
        factor_of = factor_of * jnp.repeat(jnp.exp(steps), dims[dim] // parts).reshape((-1,) + (1,) * (len(dims) - 1 - dim))
    return factor_of


def scatter_about(key, dims, spread, bound, shards=(), kind=jnp.bfloat16):
    result = jax.random.normal(key, dims, jnp.float32) * spread
    if len(shards) > 0:
        result = level_of(key, dims, shards, -0.22, 0.18) * result
    return jnp.clip(result, min=-bound, max=bound).astype(kind)


def setup_inputs(seed: int = 0) -> dict:
    streams_of = jax.random.split(jax.random.key(seed), 6)
    return {
        "solved": scatter_about(streams_of[0], (K0, N), 1.0, 6.0, ((0, 4), (1, 8))),
        "factor_rows": scatter_about(streams_of[1], (B, K0), K0 ** -0.5, 0.09375, ((1, 4),)),
        "diag_inverse": draw_diag_inverse(jax.random.fold_in(streams_of[5], 71), 0),
        "features": scatter_about(streams_of[3], (N, B), 1.0, 6.0, ((0, 8),)),
        "covariance": scatter_about(streams_of[4], (N, N), 1.0, 6.0, ((0, 8), (1, 4)), jnp.float32),
    }


def reference(solved, factor_rows, diag_inverse, features, covariance):
    high = lax.Precision.HIGHEST
    summed = jnp.dot(solved.astype(jnp.float32).T, factor_rows.astype(jnp.float32).T, precision=high)
    residual = (features.astype(jnp.float32) - summed).astype(jnp.bfloat16)
    panel = jnp.dot(residual.astype(jnp.float32), diag_inverse.astype(jnp.float32).T, precision=high).astype(jnp.bfloat16)
    wide = panel.astype(jnp.float32)
    return covariance + jnp.dot(wide, wide.T, precision=high)
```

```python
import jax
import jax.numpy as jnp
from jax import lax
from jax.sharding import PartitionSpec as P

CORES = 2
CHUNKS = 2


def tables(rows, cols):
    spans = cols // CORES
    groups = rows // cols
    flat = lambda r, c: r * cols + c
    everyone = [(r, c) for r in range(rows) for c in range(cols)]
    swap = [(flat(r, c), flat(r, c ^ 1)) for r, c in everyone]
    across = []
    bit = 1
    while bit < spans:
        across.append([(flat(r, c), flat(r, ((c // CORES) ^ bit) * CORES + c % CORES)) for r, c in everyone])
        bit *= 2
    deal = []
    for turn in range(CORES):
        pairs = []
        for r, c in everyone:
            band, member = r // groups, r % groups
            x, k = c // CORES, c % CORES
            twist = band ^ (band >> 1)
            pair = (x - twist) % spans
            target = pair * CORES + (k + turn) % CORES
            pairs.append((flat(r, c), flat(target * groups + member, band)))
        deal.append(pairs)
    share = []
    for shift in range(1, groups):
        share.append([(flat(r, c), flat(r // groups * groups + (r + shift) % groups, c)) for r, c in everyone])
    return swap, across, deal, share


def nt(a, b):
    return lax.dot_general(a, b, (((1,), (1,)), ((), ())), preferred_element_type=jnp.float32)


def body(solved, factor_rows, diag_inverse, features, covariance):
    axes = ("row", "col")
    rows, cols = lax.axis_size("row"), lax.axis_size("col")
    groups = rows // cols
    swap, across, deal, share = tables(rows, cols)
    send = lambda value, pairs: lax.ppermute(value, axes, pairs)
    row, col = lax.axis_index("row"), lax.axis_index("col")
    core, band, member = col % CORES, row // groups, row % groups
    frames = features.shape[0]
    half = frames // CORES
    step = half // CHUNKS
    partial = lax.dot_general(
        solved, factor_rows, (((0,), (1,)), ((), ())), preferred_element_type=jnp.float32
    )
    own_panels, other_panels = [], []
    col_panel = jnp.zeros((groups * frames, features.shape[1]), jnp.bfloat16)
    for index in range(CHUNKS):
        mine = core * half + index * step
        yours = (1 - core) * half + index * step
        cut = lambda array, start: lax.dynamic_slice_in_dim(array, start, step, 0)
        total = cut(partial, mine) + send(cut(partial, yours), swap)
        for pairs in across:
            total = total + send(total.astype(jnp.float16), pairs).astype(jnp.float32)
        residual = (cut(features, mine).astype(jnp.float32) - total).astype(jnp.bfloat16)
        panel = nt(residual, diag_inverse).astype(jnp.bfloat16)
        own_panels.append(panel)
        other_panels.append(send(panel, swap))
        for turn in range(CORES):
            piece = send(panel, deal[turn])
            part = (band + turn) % CORES
            parts = [(piece, member)]
            for shift, pairs in enumerate(share, 1):
                parts.append((send(piece, pairs), (member - shift) % groups))
            for value, who in parts:
                start = who * frames + part * half + index * step
                col_panel = lax.dynamic_update_slice_in_dim(col_panel, value, start, 0)
    own, other = jnp.concatenate(own_panels), jnp.concatenate(other_panels)
    row_panel = jnp.where(core == 0, jnp.concatenate([own, other]), jnp.concatenate([other, own]))
    return covariance + nt(row_panel, col_panel)


def solution(mesh):
    placed = (P("col", "row"), P(None, "col"), P(), P("row", None), P("row", "col"))
    return jax.shard_map(
        body, mesh=mesh, in_specs=placed, out_specs=P("row", "col"), check_vma=False
    )
```
